512 devices in a mesh: ctx: 128 (over x, z, core), head: 4 (over y).
Axes of the slice: x: 4, y: 4, z: 16, core: 2. Of those that a mesh axis runs over, the one named last changes fastest.
Arguments:
- query: bfloat16 [16384, 2048], P('ctx', 'head'), may hold values from -5 to 5, as said below
- key: bfloat16 [16384, 128], P('ctx'), may hold values from -5 to 5, as said below
- value: bfloat16 [16384, 128], P('ctx'), may hold values from -6 to 6
- grad_out: bfloat16 [16384, 2048], P('ctx', 'head'), may hold values from -6 to 6
- doc_lengths: int32 [32], replicated, may hold values from 1 to 1024, 16384 in all
Outputs:
- attention_out: bfloat16 [16384, 2048], P('ctx', 'head')
- grad_query: bfloat16 [16384, 2048], P('ctx', 'head')
- grad_key: bfloat16 [16384, 128], P('ctx')
- grad_value: bfloat16 [16384, 128], P('ctx')
The draws below stay inside these ranges and needn't reach their ends.
Inputs may be any that keep to these rules, and one draw needn't show every extreme that they name: `doc_lengths`: positive lengths of the documents in sequence order, summing to 16384; the longest is exactly 1024. `query`: real values. `key`: real values.
All inputs are finite; a program needn't handle non-finite values.
Results may differ from the reference program's by a relative error of at most 0.014.
Values may be sent and summed in bfloat16 or wider, within the bound.
No kernel may reach another device: no remote copies, remote signals or barrier semaphores. Data moves between devices by JAX's collectives and lax.ppermute only.
A program may use at most 64 MiB of HBM per device.

```python
import math
import jax
import jax.numpy as jnp
import numpy as np
from jax import lax

HD = 128
HEADS = 16
STRETCH = 64
DOCS = 32
REACH = 16
TOK_DEV = 128
TOKENS = 16384
MOST = 1024
N_CTX = 128


def draw_query(key, part):
    base = jax.random.fold_in(key, 11)
    result = jnp.clip(jax.random.normal(base, (TOKENS, HEADS * HD), jnp.float32), -5.0, 5.0)
    return result.astype(jnp.bfloat16)


def draw_key(key, part):
    base = jax.random.fold_in(key, 23)
    result = jnp.clip(jax.random.normal(base, (TOKENS, HD), jnp.float32), -5.0, 5.0)
    return result.astype(jnp.bfloat16)


def level_of(stream_key, dims, split, least, high):
    factor_of = 1.0
    for position, shards_of in split:
        heights = jax.random.uniform(jax.random.fold_in(jax.random.fold_in(stream_key, 6), position), (shards_of,), jnp.float32, least / len(split), high / len(split))
        factor_of = factor_of * jnp.repeat(jnp.exp(heights), dims[position] // shards_of).reshape((-1,) + (1,) * (len(dims) - 1 - position))
    return factor_of


def length_profile(amount, total, most, lean):
    loads = [(1 << 20) // math.isqrt(rank ** lean) + 1 for rank in range(2, amount + 1)]
    surplus, given = total - most - (amount - 1), [1] * (amount - 1)
    while surplus > 0:
        movable = [i for i in range(amount - 1) if given[i] < most]
        whole, left = sum([loads[i] for i in movable]), surplus
        for i in movable:
            more = min(most - given[i], max(1, left * loads[i] // whole), surplus)
            given[i] = given[i] + more
            surplus = surplus - more
    return np.array([most] + given)


def uneven_parts(rng, number_of, total, most, slope):
    if number_of == 2:
        one = jax.random.randint(rng, (), max(1, total - most), min(most, total - 1) + 1)
        return jnp.stack([one, total - one])
    tallies = jnp.asarray(length_profile(number_of, total, most, slope), jnp.int32)
    couples = (number_of - 1) // 2
    giver, taker = tallies[1:1 + 2 * couples:2], tallies[2:2 + 2 * couples:2]
    room = jnp.minimum(giver - 1, most - taker)
    shifted = jax.random.randint(jax.random.fold_in(rng, 1), (couples,), 0, 1 << 20) % (room + 1)
    tallies = tallies.at[1:1 + 2 * couples:2].set(giver - shifted).at[2:2 + 2 * couples:2].set(taker + shifted)
    return tallies[jax.random.permutation(jax.random.fold_in(rng, 2), number_of)]


def centred(key, extent, scale, reach, split=(), kind=jnp.bfloat16):
    drawn = scale * jax.random.normal(key, extent, jnp.float32)
    if split:
        drawn = drawn * level_of(key, extent, split, -0.22, 0.18)
    return jnp.clip(drawn, -reach, reach).astype(kind)


def setup_inputs(seed: int = 0) -> dict:
    arg_keys = jax.random.split(jax.random.key(seed), 6)
    query = draw_query(jax.random.fold_in(arg_keys[5], 71), 0)
    key = draw_key(jax.random.fold_in(arg_keys[5], 71), 0)
    value = centred(arg_keys[2], (TOKENS, HD), 1.0, 6.0, ((0, 128),))
    grad_out = centred(arg_keys[3], (TOKENS, HEADS * HD), 1.0, 6.0, ((0, 128), (1, 4)))
    doc_lengths = uneven_parts(arg_keys[4], DOCS, TOKENS, MOST, 2).astype(jnp.int32)
    return {"query": query, "key": key, "value": value, "grad_out": grad_out, "doc_lengths": doc_lengths}


def reference(query, key, value, grad_out, doc_lengths):
    seq_index = jnp.arange(TOKENS, dtype=jnp.int32)
    stretch_id = seq_index // STRETCH
    lower_half = stretch_id < N_CTX
    device_id = jnp.where(lower_half, stretch_id, 2 * N_CTX - 1 - stretch_id)
    shard_row = device_id * TOK_DEV + jnp.where(lower_half, 0, STRETCH) + seq_index % STRETCH
    local_row = seq_index % TOK_DEV
    owner_dev = seq_index // TOK_DEV
    back_stretch = jnp.where(local_row < STRETCH, owner_dev, 2 * N_CTX - 1 - owner_dev)
    back_pos = (back_stretch * STRETCH + local_row % STRETCH).astype(jnp.int32)
    queries = jnp.take(query, shard_row, axis=0).reshape(TOKENS, HEADS, HD)
    cotangent = jnp.take(grad_out, shard_row, axis=0).reshape(TOKENS, HEADS, HD)
    keys = jnp.take(key, shard_row, axis=0)
    values_seq = jnp.take(value, shard_row, axis=0)
    doc_ends = jnp.cumsum(doc_lengths).astype(jnp.int32)
    doc_ids = jnp.sum((doc_ends[None, :] <= seq_index[:, None]).astype(jnp.int32), axis=1)
    margin = REACH * STRETCH
    window = margin + STRETCH
    key_pad = jnp.concatenate([jnp.zeros((margin, HD), key.dtype), keys], axis=0)
    value_pad = jnp.concatenate([jnp.zeros((margin, HD), value.dtype), values_seq], axis=0)
    doc_pad = jnp.concatenate([jnp.full((margin,), -1, jnp.int32), doc_ids], axis=0)
    score_scale = HD ** -0.5

    def stretch_step(carry, stretch_index):
        grad_k_acc, grad_v_acc = carry
        start = (stretch_index * STRETCH).astype(jnp.int32)
        q_block = lax.dynamic_slice_in_dim(queries, start, STRETCH, 0).astype(jnp.float32)
        dout_block = lax.dynamic_slice_in_dim(cotangent, start, STRETCH, 0).astype(jnp.float32)
        q_docs = lax.dynamic_slice_in_dim(doc_ids, start, STRETCH, 0)
        q_pos = start + jnp.arange(STRETCH, dtype=jnp.int32)
        k_block = lax.dynamic_slice_in_dim(key_pad, start, window, 0).astype(jnp.float32)
        v_block = lax.dynamic_slice_in_dim(value_pad, start, window, 0).astype(jnp.float32)
        k_docs = lax.dynamic_slice_in_dim(doc_pad, start, window, 0)
        k_pos = start - margin + jnp.arange(window, dtype=jnp.int32)
        live_mask = (k_docs[None, :] == q_docs[:, None]) & (k_pos[None, :] <= q_pos[:, None]) & (k_pos[None, :] >= 0)
        live_mask = live_mask[None]
        scores = jnp.einsum("qhd,kd->hqk", q_block, k_block) * score_scale
        row_max = jnp.max(jnp.where(live_mask, scores, -1e30), axis=2)
        row_sum = jnp.sum(jnp.where(live_mask, jnp.exp(scores - row_max[:, :, None]), 0.0), axis=2)
        log_sum = row_max + jnp.log(row_sum)
        weights = jnp.where(live_mask, jnp.exp(scores - log_sum[:, :, None]), 0.0)
        probs = lax.optimization_barrier(weights.astype(jnp.bfloat16)).astype(jnp.float32)
        out_block = jnp.einsum("hqk,kd->qhd", probs, v_block).astype(jnp.bfloat16)
        delta = jnp.sum(dout_block * out_block.astype(jnp.float32), axis=2).T
        dprobs = jnp.einsum("qhd,kd->hqk", dout_block, v_block)
        dscores = (weights * (dprobs - delta[:, :, None]) * score_scale).astype(jnp.bfloat16)
        dscores = lax.optimization_barrier(dscores).astype(jnp.float32)
        q_grad = jnp.einsum("hqk,kd->qhd", dscores, k_block).astype(jnp.bfloat16)
        k_grad = jnp.einsum("hqk,qhd->kd", dscores, q_block)
        v_grad = jnp.einsum("hqk,qhd->kd", probs, dout_block)
        grad_k_acc = lax.dynamic_update_slice_in_dim(grad_k_acc, lax.dynamic_slice_in_dim(grad_k_acc, start, window, 0) + k_grad, start, 0)
        grad_v_acc = lax.dynamic_update_slice_in_dim(grad_v_acc, lax.dynamic_slice_in_dim(grad_v_acc, start, window, 0) + v_grad, start, 0)
        return (grad_k_acc, grad_v_acc), (out_block, q_grad)

    start_acc = jnp.zeros((TOKENS + margin, HD), jnp.float32)
    (grad_k_acc, grad_v_acc), (out_blocks, q_grads) = lax.scan(stretch_step, (start_acc, start_acc), jnp.arange(TOKENS // STRETCH, dtype=jnp.int32))
    attention_seq = out_blocks.reshape(TOKENS, HEADS * HD)
    grad_q_seq = q_grads.reshape(TOKENS, HEADS * HD)
    grad_k_seq = grad_k_acc[margin:].astype(jnp.bfloat16)
    grad_v_seq = grad_v_acc[margin:].astype(jnp.bfloat16)
    return (jnp.take(attention_seq, back_pos, axis=0), jnp.take(grad_q_seq, back_pos, axis=0),
            jnp.take(grad_k_seq, back_pos, axis=0), jnp.take(grad_v_seq, back_pos, axis=0))
```

```python
import jax
import jax.numpy as jnp
from jax import lax
from jax.experimental import pallas as pl
from jax.experimental.pallas import tpu as pltpu
from jax.sharding import PartitionSpec as P

HD = 128
STRETCH = 64
N_CTX = 128
N_HEAD = 4
LAST = 2 * N_CTX - 1
NEAR = 2
FAR = 6
GROUP = 3 * STRETCH
SIDE = 3 * GROUP
KEYS = 2 * SIDE
COLS = 2 * N_HEAD * STRETCH
DOCS = 32
NEG = -1e30
SCALE = HD**-0.5
LOG2E = 1.4426950408889634
NT = (((1,), (1,)), ((), ()))
NN = (((1,), (0,)), ((), ()))
BOTH = ("ctx", "head")


def home(stretch, copy):
    if stretch < N_CTX:
        return stretch * N_HEAD + copy
    return (LAST - stretch) * N_HEAD + N_HEAD - 1 - copy


def along(array, by):
    pairs = [
        (home(s, copy), home(s + by, copy))
        for s in range(LAST + 1)
        if 0 <= s + by <= LAST
        for copy in range(2)
    ]
    return lax.ppermute(array, BOTH, pairs)


def across(array):
    pairs = [
        (i * N_HEAD + h, i * N_HEAD + N_HEAD - 1 - h) for i in range(N_CTX) for h in range(N_HEAD)
    ]
    return lax.ppermute(array, BOTH, pairs)


def beside(array):
    pairs = [(i * N_HEAD + h, (i ^ 1) * N_HEAD + h) for i in range(N_CTX) for h in range(N_HEAD)]
    return lax.ppermute(array, BOTH, pairs)


def attend(
    docs_ref, window_ref, query_ref, grad_ref, far_ref,
    out_ref, dq_ref, far_out_ref, keep_ref, send_ref,
    q_sc, do_sc, s_sc, e_sc,
):
    index = lax.axis_index("ctx")
    lower = lax.axis_index("head") < N_HEAD // 2
    core = index % 2
    stretch = jnp.where(lower, index, LAST - index)
    first = jnp.where(lower, index - core, LAST - index + core)
    bases = (first, jnp.where(lower, first + 1, first - 1))
    rows = pl.ds(pl.multiple_of(jnp.where(lower, 0, STRETCH), STRETCH), STRETCH)
    for h in range(N_HEAD):
        part = slice(h * HD, (h + 1) * HD)
        own = slice(h * STRETCH, (h + 1) * STRETCH)
        far = slice((h + N_HEAD) * STRETCH, (h + N_HEAD + 1) * STRETCH)
        q_sc[own, :] = query_ref[rows, part]
        do_sc[own, :] = grad_ref[rows, part]
        q_sc[far, :] = far_ref[:STRETCH, part]
        do_sc[far, :] = far_ref[STRETCH:, part]
    place = stretch * STRETCH + lax.broadcasted_iota(jnp.int32, (8, COLS), 1) % STRETCH
    begin = jnp.zeros((8, COLS), jnp.int32)
    end = jnp.int32(0)
    for k in range(DOCS):
        end = end + docs_ref[k]
        begin = jnp.where(place >= end, end, begin)
    place = place[:1]
    begin = begin[:1]
    inner = lax.broadcasted_iota(jnp.int32, (STRETCH, COLS), 0)

    groups = [(side, k) for side in range(2) for k in range(3)]
    q = q_sc[...]
    peak = jnp.full((1, COLS), NEG, jnp.float32)
    for side, k in groups:
        at = side * SIDE + k * GROUP
        raw = lax.dot_general(
            window_ref[at : at + GROUP, :HD], q, NT, preferred_element_type=jnp.float32
        )
        for j in range(3):
            base = (bases[side] - NEAR * k - FAR * j) * STRETCH
            live = inner >= begin - base
            if k == 0 and j == 0:
                live = live & (inner <= place - base)
            block = jnp.where(live, raw[j * STRETCH : (j + 1) * STRETCH], NEG)
            s_sc[at + j * STRETCH : at + (j + 1) * STRETCH, :] = block
            peak = jnp.maximum(peak, jnp.max(block, axis=0, keepdims=True))
    total = jnp.zeros((1, COLS), jnp.float32)
    for side, k in groups:
        at = side * SIDE + k * GROUP
        e = jnp.exp2((s_sc[at : at + GROUP, :] - peak) * (SCALE * LOG2E))
        total = total + jnp.sum(e, axis=0, keepdims=True)
        e_sc[at : at + GROUP, :] = e.astype(jnp.bfloat16)
    share = 1.0 / total

    do = do_sc[...]
    out_t = lax.dot_general(
        window_ref[:, HD:].T, e_sc[...], NN, preferred_element_type=jnp.float32
    )
    out_t = (out_t * share).astype(jnp.bfloat16)
    out = out_t.T
    delta = jnp.sum(
        out_t.astype(jnp.float32) * do.T.astype(jnp.float32), axis=0, keepdims=True
    )
    share_rows = jnp.broadcast_to(share, (HD, COLS)).T
    do_n = (do.astype(jnp.float32) * share_rows).astype(jnp.bfloat16)
    q_n = (q.astype(jnp.float32) * (share_rows * SCALE)).astype(jnp.bfloat16)
    for k in range(3):
        grads = []
        for side in range(2):
            at = side * SIDE + k * GROUP
            e = e_sc[at : at + GROUP, :]
            dp = lax.dot_general(
                window_ref[at : at + GROUP, HD:], do, NT, preferred_element_type=jnp.float32
            )
            ds = (e.astype(jnp.float32) * (dp - delta)).astype(jnp.bfloat16)
            dk = lax.dot_general(ds, q_n, NN, preferred_element_type=jnp.float32)
            dv = lax.dot_general(e, do_n, NN, preferred_element_type=jnp.float32)
            grads.append(jnp.concatenate([dk, dv], axis=1))
            e_sc[at : at + GROUP, :] = ds
        span = slice(k * GROUP, (k + 1) * GROUP)
        keep_ref[span, :] = jnp.where(core == 0, grads[0], grads[1]).astype(jnp.bfloat16)
        send_ref[span, :] = jnp.where(core == 0, grads[1], grads[0]).astype(jnp.bfloat16)
    dq_t = lax.dot_general(
        window_ref[:, :HD].T, e_sc[...], NN, preferred_element_type=jnp.float32
    )
    dq = (dq_t * (share * SCALE)).astype(jnp.bfloat16).T
    for h in range(N_HEAD):
        part = slice(h * HD, (h + 1) * HD)
        own = slice(h * STRETCH, (h + 1) * STRETCH)
        far = slice((h + N_HEAD) * STRETCH, (h + N_HEAD + 1) * STRETCH)
        out_ref[:, part] = out[own]
        dq_ref[:, part] = dq[own]
        far_out_ref[:STRETCH, part] = out[far]
        far_out_ref[STRETCH:, part] = dq[far]


def attention(docs, window, query, grad, far):
    half = jax.ShapeDtypeStruct((STRETCH, N_HEAD * HD), jnp.bfloat16)
    both = jax.ShapeDtypeStruct((2 * STRETCH, N_HEAD * HD), jnp.bfloat16)
    side = jax.ShapeDtypeStruct((SIDE, 2 * HD), jnp.bfloat16)
    vmem = pl.BlockSpec(memory_space=pltpu.VMEM)
    return pl.pallas_call(
        attend,
        out_shape=(half, half, both, side, side),
        in_specs=[pl.BlockSpec(memory_space=pltpu.SMEM)] + [vmem] * 4,
        out_specs=(vmem,) * 5,
        scratch_shapes=[
            pltpu.VMEM((COLS, HD), jnp.bfloat16),
            pltpu.VMEM((COLS, HD), jnp.bfloat16),
            pltpu.VMEM((KEYS, COLS), jnp.float32),
            pltpu.VMEM((KEYS, COLS), jnp.bfloat16),
        ],
        cost_estimate=pl.CostEstimate(
            flops=12 * KEYS * COLS * HD,
            bytes_accessed=3 * KEYS * HD * 4,
            transcendentals=KEYS * COLS,
        ),
    )(docs, window, query, grad, far)


def body(query, key, value, grad_out, doc_lengths):
    lower = lax.axis_index("head") < N_HEAD // 2
    mine = jnp.where(lower, 0, STRETCH)
    other = STRETCH - mine

    def pick(array, first):
        return lax.dynamic_slice_in_dim(array, first, STRETCH, 0)

    far = across(jnp.concatenate([pick(query, other), pick(grad_out, other)], axis=0))
    own = jnp.concatenate([pick(key, mine), pick(value, mine)], axis=1)
    strided = jnp.concatenate([own, along(own, FAR), along(own, 2 * FAR)], axis=0)
    parity = jnp.concatenate([strided, along(strided, NEAR), along(strided, 2 * NEAR)], axis=0)
    pairs = [[i, i + 1] for i in range(0, N_CTX, 2)]
    window = lax.all_gather(parity, "ctx", axis_index_groups=pairs, axis=0, tiled=True)

    out, dq, far_out, keep, send = attention(doc_lengths, window, query, grad_out, far)

    came = beside(send)
    back = across(far_out)

    def joined(span):
        return keep[span].astype(jnp.float32) + came[span].astype(jnp.float32)

    def wide(array):
        return array.astype(jnp.float32)

    near = along(joined(slice(GROUP, 2 * GROUP)).astype(jnp.bfloat16), -NEAR)
    nearer = along(joined(slice(2 * GROUP, SIDE)).astype(jnp.bfloat16), -2 * NEAR)
    strided = joined(slice(0, GROUP)) + wide(near) + wide(nearer)
    first = along(strided[STRETCH : 2 * STRETCH].astype(jnp.bfloat16), -FAR)
    second = along(strided[2 * STRETCH :].astype(jnp.bfloat16), -2 * FAR)
    total = (strided[:STRETCH] + wide(first) + wide(second)).astype(jnp.bfloat16)
    shared = lax.all_to_all(
        jnp.broadcast_to(total, (N_HEAD,) + total.shape), "head", 0, 0
    ).astype(jnp.float32)
    kv = jnp.concatenate([shared[0] + shared[1], shared[2] + shared[3]], axis=0)
    kv = kv.astype(jnp.bfloat16)

    def placed(here, there):
        return jnp.where(
            lower, jnp.concatenate([here, there]), jnp.concatenate([there, here])
        )

    return (
        placed(out, back[:STRETCH]),
        placed(dq, back[STRETCH:]),
        kv[:, :HD],
        kv[:, HD:],
    )


def solution(mesh):
    in_specs = (P("ctx", "head"), P("ctx", None), P("ctx", None), P("ctx", "head"), P())
    out_specs = (P("ctx", "head"), P("ctx", "head"), P("ctx", None), P("ctx", None))
    return jax.shard_map(body, mesh=mesh, in_specs=in_specs, out_specs=out_specs, check_vma=False)
```

```python
import jax
import jax.numpy as jnp
from jax import lax
from jax.experimental import pallas as pl
from jax.experimental.pallas import tpu as pltpu
from jax.sharding import PartitionSpec as P


HD = 128
STRETCH = 64
N_CTX = 128
N_HEAD = 4
LAST = 2 * N_CTX - 1
CHIP = 2
OFFSETS = (0, 4, 2, 6, 1, 5, 3, 7, 8)
GROUP = 3 * STRETCH
SIDE = 9 * STRETCH
COLS = 2 * N_HEAD * STRETCH
DOCS = 32
NEG = -1e30
SCALE = HD**-0.5
LOG2E = 1.4426950408889634
NT = (((1,), (1,)), ((), ()))
NN = (((1,), (0,)), ((), ()))
BOTH = ("ctx", "head")
PAIRS = [[i, i + 1] for i in range(0, N_CTX, 2)]


def home(stretch, copy):
    if stretch < N_CTX:
        return stretch * N_HEAD + copy
    return (LAST - stretch) * N_HEAD + N_HEAD - 1 - copy


def along(array, by):
    pairs = [
        (home(s, copy), home(s + by, copy))
        for s in range(LAST + 1)
        if 0 <= s + by <= LAST
        for copy in range(2)
    ]
    return lax.ppermute(array, BOTH, pairs)


def across(array):
    pairs = [
        (i * N_HEAD + h, i * N_HEAD + N_HEAD - 1 - h) for i in range(N_CTX) for h in range(N_HEAD)
    ]
    return lax.ppermute(array, BOTH, pairs)


def place_of():
    index = lax.axis_index("ctx")
    lower = lax.axis_index("head") < N_HEAD // 2
    core = index % 2
    first = jnp.where(lower, index - core, LAST - index + core)
    return core, lower, (first, jnp.where(lower, first + 1, first - 1))


def prepare(docs_ref, query_ref, grad_ref, far_ref, both_ref, begin_ref):
    _, lower, stretches = place_of()
    rows = pl.ds(pl.multiple_of(jnp.where(lower, 0, STRETCH), STRETCH), STRETCH)
    for h in range(N_HEAD):
        part = slice(h * HD, (h + 1) * HD)
        own = h * STRETCH
        far = (h + N_HEAD) * STRETCH
        both_ref[own : own + STRETCH, :] = query_ref[rows, part]
        both_ref[far : far + STRETCH, :] = far_ref[:STRETCH, part]
        own, far = own + COLS, far + COLS
        both_ref[own : own + STRETCH, :] = grad_ref[rows, part]
        both_ref[far : far + STRETCH, :] = far_ref[STRETCH:, part]
    inner = lax.broadcasted_iota(jnp.int32, (8, COLS), 1) % STRETCH
    for side in range(2):
        place = stretches[side] * STRETCH + inner
        begin = jnp.zeros((8, COLS), jnp.int32)
        end = jnp.int32(0)
        for k in range(DOCS):
            end = end + docs_ref[k]
            begin = jnp.where(place >= end, end, begin)
        begin_ref[:, side * COLS : (side + 1) * COLS] = begin


def score(window_ref, both_ref, begin_ref, e_ref, dp_ref, stats_ref, s_sc):
    core, _, stretches = place_of()
    mine = jnp.where(core == 0, stretches[0], stretches[1])
    inner = lax.broadcasted_iota(jnp.int32, (STRETCH, COLS), 0)
    row = lax.broadcasted_iota(jnp.int32, (1, COLS), 1) % STRETCH
    for side in range(2):
        columns = slice(side * COLS, (side + 1) * COLS)
        q = both_ref[2 * side * COLS : (2 * side + 1) * COLS, :]
        do = both_ref[(2 * side + 1) * COLS : (2 * side + 2) * COLS, :]
        place = stretches[side] * STRETCH + row
        begin = begin_ref[:1, columns]
        peak = jnp.full((1, COLS), NEG, jnp.float32)
        for k in range(3):
            at = k * GROUP
            raw = lax.dot_general(
                window_ref[at : at + GROUP, :HD], q, NT, preferred_element_type=jnp.float32
            )
            for j in range(3):
                base = (mine - CHIP * OFFSETS[3 * k + j]) * STRETCH
                live = inner >= begin - base
                if k == 0 and j == 0:
                    live = live & (inner <= place - base)
                block = jnp.where(live, raw[j * STRETCH : (j + 1) * STRETCH], NEG)
                s_sc[at + j * STRETCH : at + (j + 1) * STRETCH, columns] = block
                peak = jnp.maximum(peak, jnp.max(block, axis=0, keepdims=True))
        total = jnp.zeros((1, COLS), jnp.float32)
        delta = jnp.zeros((1, COLS), jnp.float32)
        for k in range(3):
            at = slice(k * GROUP, (k + 1) * GROUP)
            e = jnp.exp2((s_sc[at, columns] - peak) * (SCALE * LOG2E))
            dp = lax.dot_general(
                window_ref[at, HD:], do, NT, preferred_element_type=jnp.float32
            )
            total = total + jnp.sum(e, axis=0, keepdims=True)
            delta = delta + jnp.sum(e * dp, axis=0, keepdims=True)
            e_ref[at, columns] = e.astype(jnp.bfloat16)
            dp_ref[at, columns] = dp
        rest = jnp.zeros((5, COLS), jnp.float32)
        stats_ref[:, columns] = jnp.concatenate([peak, total, delta, rest], axis=0)


def grads(window_ref, both_ref, e_ref, dp_ref, stats_ref, grad_ref, en_ref, ds_ref):
    core = lax.axis_index("ctx") % 2
    for k in range(3):
        at = slice(k * GROUP, (k + 1) * GROUP)
        dk = jnp.zeros((GROUP, HD), jnp.float32)
        dv = jnp.zeros((GROUP, HD), jnp.float32)
        for side in range(2):
            columns = slice(side * COLS, (side + 1) * COLS)
            q = both_ref[2 * side * COLS : (2 * side + 1) * COLS, :]
            do = both_ref[(2 * side + 1) * COLS : (2 * side + 2) * COLS, :]
            peaks = stats_ref[0:1, columns], stats_ref[8:9, columns]
            peak = jnp.maximum(*peaks)
            scales = [jnp.exp2((p - peak) * (SCALE * LOG2E)) for p in peaks]
            total = scales[0] * stats_ref[1:2, columns] + scales[1] * stats_ref[9:10, columns]
            delta = scales[0] * stats_ref[2:3, columns] + scales[1] * stats_ref[10:11, columns]
            delta = delta / total
            share = jnp.where(core == 0, scales[0], scales[1]) / total
            e = e_ref[at, columns].astype(jnp.float32) * share
            en = e.astype(jnp.bfloat16)
            ds = (e * (dp_ref[at, columns] - delta)).astype(jnp.bfloat16)
            dk = dk + lax.dot_general(ds, q, NN, preferred_element_type=jnp.float32)
            dv = dv + lax.dot_general(en, do, NN, preferred_element_type=jnp.float32)
            en_ref[at, columns] = en
            ds_ref[at, columns] = ds
        grad_ref[at, :HD] = (dk * SCALE).astype(jnp.bfloat16)
        grad_ref[at, HD:] = dv.astype(jnp.bfloat16)


def partial(window_ref, en_ref, ds_ref, keep_ref, send_ref):
    core = lax.axis_index("ctx") % 2
    out = lax.dot_general(
        window_ref[:, HD:].T, en_ref[...], NN, preferred_element_type=jnp.float32
    )
    dq = SCALE * lax.dot_general(
        window_ref[:, :HD].T, ds_ref[...], NN, preferred_element_type=jnp.float32
    )
    for at, both in ((0, out), (HD, dq)):
        one, two = both[:, :COLS], both[:, COLS:]
        keep_ref[at : at + HD, :] = jnp.where(core == 0, one, two)
        send_ref[at : at + HD, :] = jnp.where(core == 0, two, one).astype(jnp.bfloat16)


def finish(sent_ref, keep_ref, out_ref, dq_ref, far_out_ref):
    core = lax.axis_index("ctx") % 2
    came = sent_ref[pl.ds(pl.multiple_of((1 - core) * 2 * HD, 2 * HD), 2 * HD), :]
    both = (keep_ref[...] + came.astype(jnp.float32)).astype(jnp.bfloat16)
    out = both[:HD].T
    dq = both[HD:].T
    for h in range(N_HEAD):
        part = slice(h * HD, (h + 1) * HD)
        own = slice(h * STRETCH, (h + 1) * STRETCH)
        far = slice((h + N_HEAD) * STRETCH, (h + N_HEAD + 1) * STRETCH)
        out_ref[:, part] = out[own]
        dq_ref[:, part] = dq[own]
        far_out_ref[:STRETCH, part] = out[far]
        far_out_ref[STRETCH:, part] = dq[far]


VMEM = pl.BlockSpec(memory_space=pltpu.VMEM)
SMEM = pl.BlockSpec(memory_space=pltpu.SMEM)
F32 = jnp.float32


def shaped(rows, columns, dtype=jnp.bfloat16):
    return jax.ShapeDtypeStruct((rows, columns), dtype)


def run(kernel, outs, args, flops, scratch=(), scalars=0):
    return pl.pallas_call(
        kernel,
        out_shape=outs,
        in_specs=[SMEM] * scalars + [VMEM] * (len(args) - scalars),
        out_specs=(VMEM,) * len(outs),
        scratch_shapes=scratch,
        compiler_params=pltpu.CompilerParams(vmem_limit_bytes=20 << 20),
        cost_estimate=pl.CostEstimate(flops=flops, bytes_accessed=8 * COLS * HD, transcendentals=0),
    )(*args)


def prepared(docs, query, grad, far):
    outs = (shaped(2 * COLS, HD), shaped(8, 2 * COLS, jnp.int32))
    return run(prepare, outs, (docs, query, grad, far), DOCS * COLS, scalars=1)


def scored(window, both, begin):
    outs = (shaped(SIDE, 2 * COLS), shaped(SIDE, 2 * COLS, F32), shaped(8, 2 * COLS, F32))
    work = 8 * SIDE * COLS * HD
    return run(score, outs, (window, both, begin), work, (pltpu.VMEM((SIDE, 2 * COLS), F32),))


def graded(window, both, e, dp, stats):
    outs = (shaped(SIDE, 2 * HD), shaped(SIDE, 2 * COLS), shaped(SIDE, 2 * COLS))
    return run(grads, outs, (window, both, e, dp, stats), 8 * SIDE * COLS * HD)


def parted(window, en, ds):
    outs = (shaped(2 * HD, COLS, F32), shaped(2 * HD, COLS))
    return run(partial, outs, (window, en, ds), 8 * SIDE * COLS * HD)


def finished(sent, keep):
    half, both = shaped(STRETCH, N_HEAD * HD), shaped(2 * STRETCH, N_HEAD * HD)
    return run(finish, (half, half, both), (sent, keep), COLS * HD)


def paired(array):
    return lax.all_gather(array, "ctx", axis_index_groups=PAIRS, axis=0, tiled=True)


def body(query, key, value, grad_out, doc_lengths):
    lower = lax.axis_index("head") < N_HEAD // 2
    mine = jnp.where(lower, 0, STRETCH)
    other = STRETCH - mine

    def pick(array, first):
        return lax.dynamic_slice_in_dim(array, first, STRETCH, 0)

    far = across(jnp.concatenate([pick(query, other), pick(grad_out, other)], axis=0))
    own = jnp.concatenate([pick(key, mine), pick(value, mine)], axis=1)
    at_4 = along(own, 4 * CHIP)
    two = jnp.concatenate([own, at_4], axis=0)
    at_2_6 = along(two, 2 * CHIP)
    at_8 = along(at_4, 4 * CHIP)
    four = jnp.concatenate([two, at_2_6], axis=0)
    odd = along(four, CHIP)
    parity = jnp.concatenate([four, odd, at_8], axis=0)
    own_rows, begin = prepared(doc_lengths, query, grad_out, far)
    both = paired(own_rows)
    e, dp, stats = scored(parity, both, begin)
    stats = paired(stats)
    grad, en, ds = graded(parity, both, e, dp, stats)
    keep, send = parted(parity, en, ds)
    out, dq, far_out = finished(paired(send), keep)

    def block(start, stop):
        return grad[start * STRETCH : stop * STRETCH]

    def home_by(array, chips):
        return along(array.astype(jnp.bfloat16), -chips * CHIP).astype(jnp.float32)

    eighth = home_by(block(8, 9), 4)
    even = block(0, 4).astype(F32) + home_by(block(4, 8), 1)
    first = even[: 2 * STRETCH] + home_by(even[2 * STRETCH :], 2)
    back = across(far_out)
    total = (first[:STRETCH] + home_by(first[STRETCH:] + eighth, 4)).astype(jnp.bfloat16)
    copies = jnp.broadcast_to(total, (N_HEAD,) + total.shape)
    shared = lax.all_to_all(copies, "head", 0, 0)
    shared = shared.astype(jnp.float32)
    kv = jnp.concatenate([shared[0] + shared[1], shared[2] + shared[3]], axis=0)
    kv = kv.astype(jnp.bfloat16)

    def placed(here, there):
        return jnp.where(
            lower, jnp.concatenate([here, there]), jnp.concatenate([there, here])
        )

    return (
        placed(out, back[:STRETCH]),
        placed(dq, back[STRETCH:]),
        kv[:, :HD],
        kv[:, HD:],
    )


def solution(mesh):
    in_specs = (P("ctx", "head"), P("ctx", None), P("ctx", None), P("ctx", "head"), P())
    out_specs = (P("ctx", "head"), P("ctx", "head"), P("ctx", None), P("ctx", None))

    return jax.shard_map(body, mesh=mesh, in_specs=in_specs, out_specs=out_specs, check_vma=False)
```

```python
import jax
import jax.numpy as jnp
from jax import lax
from jax.experimental import pallas as pl
from jax.experimental.pallas import tpu as pltpu
from jax.sharding import PartitionSpec as P


HD = 128
STRETCH = 64
N_CTX = 128
N_HEAD = 4
LAST = 2 * N_CTX - 1
CHIP = 2
OFFSETS = (0, 4, 2, 6, 1, 5, 3, 7, 8)
GROUP = 3 * STRETCH
SIDE = 9 * STRETCH
COLS = 2 * N_HEAD * STRETCH
DOCS = 32
NEG = -1e30
SCALE = HD**-0.5
LOG2E = 1.4426950408889634
NT = (((1,), (1,)), ((), ()))
NN = (((1,), (0,)), ((), ()))
BOTH = ("ctx", "head")
PAIRS = [[i, i + 1] for i in range(0, N_CTX, 2)]


def home(stretch, copy):
    if stretch < N_CTX:
        return stretch * N_HEAD + copy
    return (LAST - stretch) * N_HEAD + N_HEAD - 1 - copy


def along(array, by):
    pairs = [
        (home(s, copy), home(s + by, copy))
        for s in range(LAST + 1)
        if 0 <= s + by <= LAST
        for copy in range(2)
    ]
    return lax.ppermute(array, BOTH, pairs)


def across(array):
    pairs = [
        (i * N_HEAD + h, i * N_HEAD + N_HEAD - 1 - h) for i in range(N_CTX) for h in range(N_HEAD)
    ]
    return lax.ppermute(array, BOTH, pairs)


def place_of():
    index = lax.axis_index("ctx")
    lower = lax.axis_index("head") < N_HEAD // 2
    core = index % 2
    first = jnp.where(lower, index - core, LAST - index + core)
    return core, lower, (first, jnp.where(lower, first + 1, first - 1))


def settle(
    out_ref, dq_ref, back_ref, kv_ref, all_out_ref, all_dq_ref, gk_ref, gv_ref, sems
):
    _, lower, _ = place_of()
    here = pl.multiple_of(jnp.where(lower, 0, STRETCH), STRETCH)
    there = pl.multiple_of(jnp.where(lower, STRETCH, 0), STRETCH)
    moves = (
        (out_ref, all_out_ref.at[pl.ds(here, STRETCH), :]),
        (back_ref.at[:STRETCH, :], all_out_ref.at[pl.ds(there, STRETCH), :]),
        (dq_ref, all_dq_ref.at[pl.ds(here, STRETCH), :]),
        (back_ref.at[STRETCH:, :], all_dq_ref.at[pl.ds(there, STRETCH), :]),
        (kv_ref.at[:, :HD], gk_ref),
        (kv_ref.at[:, HD:], gv_ref),
    )
    copies = [pltpu.make_async_copy(a, b, sems.at[i]) for i, (a, b) in enumerate(moves)]
    for copy in copies:
        copy.start()
    for copy in copies:
        copy.wait()


def prepare(docs_ref, query_ref, grad_ref, far_ref, both_ref, begin_ref):
    _, lower, stretches = place_of()
    rows = pl.ds(pl.multiple_of(jnp.where(lower, 0, STRETCH), STRETCH), STRETCH)
    for h in range(N_HEAD):
        part = slice(h * HD, (h + 1) * HD)
        beyond = slice((h + N_HEAD) * HD, (h + N_HEAD + 1) * HD)
        own = h * STRETCH
        far = (h + N_HEAD) * STRETCH
        both_ref[own : own + STRETCH, :] = query_ref[rows, part]
        both_ref[far : far + STRETCH, :] = far_ref[:, part]
        own, far = own + COLS, far + COLS
        both_ref[own : own + STRETCH, :] = grad_ref[rows, part]
        both_ref[far : far + STRETCH, :] = far_ref[:, beyond]
    inner = lax.broadcasted_iota(jnp.int32, (8, COLS), 1) % STRETCH
    for side in range(2):
        place = stretches[side] * STRETCH + inner
        begin = jnp.zeros((8, COLS), jnp.int32)
        end = jnp.int32(0)
        for k in range(DOCS):
            end = end + docs_ref[k]
            begin = jnp.where(place >= end, end, begin)
        begin_ref[:, side * COLS : (side + 1) * COLS] = begin


def score(window_ref, both_ref, begin_ref, e_ref, dp_ref, stats_ref, s_sc):
    core, _, stretches = place_of()
    mine = jnp.where(core == 0, stretches[0], stretches[1])
    inner = lax.broadcasted_iota(jnp.int32, (STRETCH, COLS), 0)
    row = lax.broadcasted_iota(jnp.int32, (1, COLS), 1) % STRETCH
    for side in range(2):
        columns = slice(side * COLS, (side + 1) * COLS)
        q = both_ref[2 * side * COLS : (2 * side + 1) * COLS, :]
        do = both_ref[(2 * side + 1) * COLS : (2 * side + 2) * COLS, :]
        place = stretches[side] * STRETCH + row
        begin = begin_ref[:1, columns]
        peak = jnp.full((1, COLS), NEG, jnp.float32)
        for k in range(3):
            at = k * GROUP
            raw = lax.dot_general(
                window_ref[at : at + GROUP, :HD], q, NT, preferred_element_type=jnp.float32
            )
            for j in range(3):
                base = (mine - CHIP * OFFSETS[3 * k + j]) * STRETCH
                live = inner >= begin - base
                if k == 0 and j == 0:
                    live = live & (inner <= place - base)
                block = jnp.where(live, raw[j * STRETCH : (j + 1) * STRETCH], NEG)
                s_sc[at + j * STRETCH : at + (j + 1) * STRETCH, columns] = block
                peak = jnp.maximum(peak, jnp.max(block, axis=0, keepdims=True))
        total = jnp.zeros((1, COLS), jnp.float32)
        delta = jnp.zeros((1, COLS), jnp.float32)
        for k in range(3):
            at = slice(k * GROUP, (k + 1) * GROUP)
            e = jnp.exp2((s_sc[at, columns] - peak) * (SCALE * LOG2E))
            dp = lax.dot_general(
                window_ref[at, HD:], do, NT, preferred_element_type=jnp.float32
            )
            total = total + jnp.sum(e, axis=0, keepdims=True)
            delta = delta + jnp.sum(e * dp, axis=0, keepdims=True)
            e_ref[at, columns] = e.astype(jnp.bfloat16)
            dp_ref[at, columns] = dp
        rest = jnp.zeros((5, COLS), jnp.float32)
        stats_ref[:, columns] = jnp.concatenate([peak, total, delta, rest], axis=0)


def grads(window_ref, both_ref, e_ref, dp_ref, stats_ref, grad_ref, en_ref, ds_ref):
    core = lax.axis_index("ctx") % 2
    for k in range(3):
        at = slice(k * GROUP, (k + 1) * GROUP)
        dk = jnp.zeros((GROUP, HD), jnp.float32)
        dv = jnp.zeros((GROUP, HD), jnp.float32)
        for side in range(2):
            columns = slice(side * COLS, (side + 1) * COLS)
            q = both_ref[2 * side * COLS : (2 * side + 1) * COLS, :]
            do = both_ref[(2 * side + 1) * COLS : (2 * side + 2) * COLS, :]
            peaks = stats_ref[0:1, columns], stats_ref[8:9, columns]
            peak = jnp.maximum(*peaks)
            scales = [jnp.exp2((p - peak) * (SCALE * LOG2E)) for p in peaks]
            total = scales[0] * stats_ref[1:2, columns] + scales[1] * stats_ref[9:10, columns]
            delta = scales[0] * stats_ref[2:3, columns] + scales[1] * stats_ref[10:11, columns]
            delta = delta / total
            share = jnp.where(core == 0, scales[0], scales[1]) / total
            e = e_ref[at, columns].astype(jnp.float32) * share
            en = e.astype(jnp.bfloat16)
            ds = (e * (dp_ref[at, columns] - delta)).astype(jnp.bfloat16)
            dk = dk + lax.dot_general(ds, q, NN, preferred_element_type=jnp.float32)
            dv = dv + lax.dot_general(en, do, NN, preferred_element_type=jnp.float32)
            en_ref[at, columns] = en
            ds_ref[at, columns] = ds
        grad_ref[at, :HD] = (dk * SCALE).astype(jnp.bfloat16)
        grad_ref[at, HD:] = dv.astype(jnp.bfloat16)


def partial(window_ref, en_ref, ds_ref, keep_ref, send_ref):
    core = lax.axis_index("ctx") % 2
    out = lax.dot_general(
        window_ref[:, HD:].T, en_ref[...], NN, preferred_element_type=jnp.float32
    )
    dq = SCALE * lax.dot_general(
        window_ref[:, :HD].T, ds_ref[...], NN, preferred_element_type=jnp.float32
    )
    for at, both in ((0, out), (HD, dq)):
        one, two = both[:, :COLS], both[:, COLS:]
        keep_ref[at : at + HD, :] = jnp.where(core == 0, one, two)
        send_ref[at : at + HD, :] = jnp.where(core == 0, two, one).astype(jnp.bfloat16)


def finish(sent_ref, keep_ref, out_ref, dq_ref, far_out_ref):
    core = lax.axis_index("ctx") % 2
    came = sent_ref[pl.ds(pl.multiple_of((1 - core) * 2 * HD, 2 * HD), 2 * HD), :]
    both = (keep_ref[...] + came.astype(jnp.float32)).astype(jnp.bfloat16)
    out = both[:HD].T
    dq = both[HD:].T
    for h in range(N_HEAD):
        part = slice(h * HD, (h + 1) * HD)
        own = slice(h * STRETCH, (h + 1) * STRETCH)
        far = slice((h + N_HEAD) * STRETCH, (h + N_HEAD + 1) * STRETCH)
        out_ref[:, part] = out[own]
        dq_ref[:, part] = dq[own]
        far_out_ref[:STRETCH, part] = out[far]
        far_out_ref[STRETCH:, part] = dq[far]


VMEM = pl.BlockSpec(memory_space=pltpu.VMEM)
SMEM = pl.BlockSpec(memory_space=pltpu.SMEM)
F32 = jnp.float32


def shaped(rows, columns, dtype=jnp.bfloat16):
    return jax.ShapeDtypeStruct((rows, columns), dtype)


def run(kernel, outs, args, flops, scratch=(), scalars=0):
    return pl.pallas_call(
        kernel,
        out_shape=outs,
        in_specs=[SMEM] * scalars + [VMEM] * (len(args) - scalars),
        out_specs=(VMEM,) * len(outs),
        scratch_shapes=scratch,
        compiler_params=pltpu.CompilerParams(vmem_limit_bytes=20 << 20),
        cost_estimate=pl.CostEstimate(flops=flops, bytes_accessed=8 * COLS * HD, transcendentals=0),
    )(*args)


def settled(*arrays):
    wide, thin = shaped(2 * STRETCH, N_HEAD * HD), shaped(2 * STRETCH, HD)
    return pl.pallas_call(
        settle,
        out_shape=(wide, wide, thin, thin),
        in_specs=[VMEM] * 4,
        out_specs=(pl.BlockSpec(memory_space=pltpu.HBM),) * 4,
        scratch_shapes=(pltpu.SemaphoreType.DMA((6,)),),
        compiler_params=pltpu.CompilerParams(vmem_limit_bytes=2 << 20),
    )(*arrays)


def prepared(docs, query, grad, far):
    outs = (shaped(2 * COLS, HD), shaped(8, 2 * COLS, jnp.int32))
    return run(prepare, outs, (docs, query, grad, far), DOCS * COLS, scalars=1)


def scored(window, both, begin):
    outs = (shaped(SIDE, 2 * COLS), shaped(SIDE, 2 * COLS, F32), shaped(8, 2 * COLS, F32))
    work = 8 * SIDE * COLS * HD
    return run(score, outs, (window, both, begin), work, (pltpu.VMEM((SIDE, 2 * COLS), F32),))


def graded(window, both, e, dp, stats):
    outs = (shaped(SIDE, 2 * HD), shaped(SIDE, 2 * COLS), shaped(SIDE, 2 * COLS))
    return run(grads, outs, (window, both, e, dp, stats), 8 * SIDE * COLS * HD)


def parted(window, en, ds):
    outs = (shaped(2 * HD, COLS, F32), shaped(2 * HD, COLS))
    return run(partial, outs, (window, en, ds), 8 * SIDE * COLS * HD)


def finished(sent, keep):
    half, both = shaped(STRETCH, N_HEAD * HD), shaped(2 * STRETCH, N_HEAD * HD)
    return run(finish, (half, half, both), (sent, keep), COLS * HD)


def paired(array, axis="ctx", groups=PAIRS):
    return lax.all_gather(array, axis, axis_index_groups=groups, axis=0, tiled=True)


def body(query, key, value, grad_out, doc_lengths):
    lower = lax.axis_index("head") < N_HEAD // 2
    mine = jnp.where(lower, 0, STRETCH)

    def pick(first, second, start):
        both = jnp.concatenate([first, second], axis=1)
        return lax.dynamic_slice_in_dim(both, start, STRETCH, 0)

    own = pick(key, value, mine)
    far = across(pick(query, grad_out, STRETCH - mine))
    at_4 = along(own, 4 * CHIP)
    two = jnp.concatenate([own, at_4], axis=0)
    at_2_6 = along(two, 2 * CHIP)
    at_8 = along(at_4, 4 * CHIP)
    four = jnp.concatenate([two, at_2_6], axis=0)
    odd = along(four, CHIP)
    parity = jnp.concatenate([four, odd, at_8], axis=0)
    own_rows, begin = prepared(doc_lengths, query, grad_out, far)
    both = paired(own_rows)
    e, dp, stats = scored(parity, both, begin)
    stats = paired(stats)
    grad, en, ds = graded(parity, both, e, dp, stats)
    keep, send = parted(parity, en, ds)
    out, dq, far_out = finished(paired(send), keep)

    def block(start, stop):
        return grad[start * STRETCH : stop * STRETCH]

    def home_by(array, chips):
        return along(array.astype(jnp.bfloat16), -chips * CHIP).astype(jnp.float32)

    eighth = home_by(block(8, 9), 4)
    even = block(0, 4).astype(F32) + home_by(block(4, 8), 1)
    first = even[: 2 * STRETCH] + home_by(even[2 * STRETCH :], 2)
    back = across(far_out)
    total = (first[:STRETCH] + home_by(first[STRETCH:] + eighth, 4)).astype(jnp.bfloat16)
    copies = paired(total, "head", [[0, 1], [2, 3]]).astype(F32)
    summed = (copies[:STRETCH] + copies[STRETCH:]).astype(jnp.bfloat16)
    kv = paired(summed, "head", [[0, 3], [1, 2]])
    return settled(out, dq, back, kv)


def solution(mesh):
    in_specs = (P("ctx", "head"), P("ctx", None), P("ctx", None), P("ctx", "head"), P())
    out_specs = (P("ctx", "head"), P("ctx", "head"), P("ctx", None), P("ctx", None))

    return jax.shard_map(body, mesh=mesh, in_specs=in_specs, out_specs=out_specs, check_vma=False)
```

```python
import jax
import jax.numpy as jnp
from jax import lax
from jax.experimental import pallas as pl
from jax.experimental.pallas import tpu as pltpu
from jax.sharding import PartitionSpec as P


HD = 128
STRETCH = 64
N_CTX = 128
N_HEAD = 4
LAST = 2 * N_CTX - 1
CHIP = 2
OFFSETS = (0, 4, 2, 6, 1, 5, 3, 7, 8)
GROUP = 3 * STRETCH
SIDE = 9 * STRETCH
COLS = 2 * N_HEAD * STRETCH
DOCS = 32
NEG = -1e30
SCALE = HD**-0.5
LOG2E = 1.4426950408889634
NT = (((1,), (1,)), ((), ()))
NN = (((1,), (0,)), ((), ()))
BOTH = ("ctx", "head")
PAIRS = [[i, i + 1] for i in range(0, N_CTX, 2)]


def home(stretch, copy):
    if stretch < N_CTX:
        return stretch * N_HEAD + copy
    return (LAST - stretch) * N_HEAD + N_HEAD - 1 - copy


def along(array, by):
    pairs = [
        (home(s, copy), home(s + by, copy))
        for s in range(LAST + 1)
        if 0 <= s + by <= LAST
        for copy in range(2)
    ]
    return lax.ppermute(array, BOTH, pairs)


def across(array):
    pairs = [
        (i * N_HEAD + h, i * N_HEAD + N_HEAD - 1 - h) for i in range(N_CTX) for h in range(N_HEAD)
    ]
    return lax.ppermute(array, BOTH, pairs)


def place_of():
    index = lax.axis_index("ctx")
    lower = lax.axis_index("head") < N_HEAD // 2
    core = index % 2
    first = jnp.where(lower, index - core, LAST - index + core)
    return core, lower, (first, jnp.where(lower, first + 1, first - 1))


def settle(
    out_ref, dq_ref, back_ref, kv_ref, all_out_ref, all_dq_ref, gk_ref, gv_ref, sems
):
    _, lower, _ = place_of()
    here = pl.multiple_of(jnp.where(lower, 0, STRETCH), STRETCH)
    there = pl.multiple_of(jnp.where(lower, STRETCH, 0), STRETCH)
    moves = (
        (out_ref, all_out_ref.at[pl.ds(here, STRETCH), :]),
        (back_ref.at[:STRETCH, :], all_out_ref.at[pl.ds(there, STRETCH), :]),
        (dq_ref, all_dq_ref.at[pl.ds(here, STRETCH), :]),
        (back_ref.at[STRETCH:, :], all_dq_ref.at[pl.ds(there, STRETCH), :]),
        (kv_ref.at[:, :HD], gk_ref),
        (kv_ref.at[:, HD:], gv_ref),
    )
    copies = [pltpu.make_async_copy(a, b, sems.at[i]) for i, (a, b) in enumerate(moves)]
    for copy in copies:
        copy.start()
    for copy in copies:
        copy.wait()


def bounds(docs_ref, begin_ref):
    _, _, stretches = place_of()
    inner = lax.broadcasted_iota(jnp.int32, (8, COLS), 1) % STRETCH
    for side in range(2):
        place = stretches[side] * STRETCH + inner
        begin = jnp.zeros((8, COLS), jnp.int32)
        end = jnp.int32(0)
        for k in range(DOCS):
            end = end + docs_ref[k]
            begin = jnp.where(place >= end, end, begin)
        begin_ref[:, side * COLS : (side + 1) * COLS] = begin


def prepare(query_ref, grad_ref, far_ref, both_ref):
    _, lower, _ = place_of()
    rows = pl.ds(pl.multiple_of(jnp.where(lower, 0, STRETCH), STRETCH), STRETCH)
    for h in range(N_HEAD):
        part = slice(h * HD, (h + 1) * HD)
        beyond = slice((h + N_HEAD) * HD, (h + N_HEAD + 1) * HD)
        own = h * STRETCH
        far = (h + N_HEAD) * STRETCH
        both_ref[own : own + STRETCH, :] = query_ref[rows, part]
        both_ref[far : far + STRETCH, :] = far_ref[:, part]
        own, far = own + COLS, far + COLS
        both_ref[own : own + STRETCH, :] = grad_ref[rows, part]
        both_ref[far : far + STRETCH, :] = far_ref[:, beyond]


def score(window_ref, both_ref, begin_ref, e_ref, dp_ref, stats_ref, s_sc):
    core, _, stretches = place_of()
    mine = jnp.where(core == 0, stretches[0], stretches[1])
    inner = lax.broadcasted_iota(jnp.int32, (STRETCH, COLS), 0)
    row = lax.broadcasted_iota(jnp.int32, (1, COLS), 1) % STRETCH
    for side in range(2):
        columns = slice(side * COLS, (side + 1) * COLS)
        q = both_ref[2 * side * COLS : (2 * side + 1) * COLS, :]
        do = both_ref[(2 * side + 1) * COLS : (2 * side + 2) * COLS, :]
        place = stretches[side] * STRETCH + row
        begin = begin_ref[:1, columns]
        peak = jnp.full((1, COLS), NEG, jnp.float32)
        for k in range(3):
            at = k * GROUP
            raw = lax.dot_general(
                window_ref[at : at + GROUP, :HD], q, NT, preferred_element_type=jnp.float32
            )
            for j in range(3):
                base = (mine - CHIP * OFFSETS[3 * k + j]) * STRETCH
                live = inner >= begin - base
                if k == 0 and j == 0:
                    live = live & (inner <= place - base)
                block = jnp.where(live, raw[j * STRETCH : (j + 1) * STRETCH], NEG)
                s_sc[at + j * STRETCH : at + (j + 1) * STRETCH, columns] = block
                peak = jnp.maximum(peak, jnp.max(block, axis=0, keepdims=True))
        total = jnp.zeros((1, COLS), jnp.float32)
        delta = jnp.zeros((1, COLS), jnp.float32)
        for k in range(3):
            at = slice(k * GROUP, (k + 1) * GROUP)
            e = jnp.exp2((s_sc[at, columns] - peak) * (SCALE * LOG2E))
            dp = lax.dot_general(
                window_ref[at, HD:], do, NT, preferred_element_type=jnp.float32
            )
            total = total + jnp.sum(e, axis=0, keepdims=True)
            delta = delta + jnp.sum(e * dp, axis=0, keepdims=True)
            e_ref[at, columns] = e.astype(jnp.bfloat16)
            dp_ref[at, columns] = dp
        rest = jnp.zeros((5, COLS), jnp.float32)
        stats_ref[:, columns] = jnp.concatenate([peak, total, delta, rest], axis=0)


def grads(window_ref, both_ref, e_ref, dp_ref, stats_ref, grad_ref, en_ref, ds_ref):
    core = lax.axis_index("ctx") % 2
    for k in range(3):
        at = slice(k * GROUP, (k + 1) * GROUP)
        dk = jnp.zeros((GROUP, HD), jnp.float32)
        dv = jnp.zeros((GROUP, HD), jnp.float32)
        for side in range(2):
            columns = slice(side * COLS, (side + 1) * COLS)
            q = both_ref[2 * side * COLS : (2 * side + 1) * COLS, :]
            do = both_ref[(2 * side + 1) * COLS : (2 * side + 2) * COLS, :]
            peaks = stats_ref[0:1, columns], stats_ref[8:9, columns]
            peak = jnp.maximum(*peaks)
            scales = [jnp.exp2((p - peak) * (SCALE * LOG2E)) for p in peaks]
            total = scales[0] * stats_ref[1:2, columns] + scales[1] * stats_ref[9:10, columns]
            delta = scales[0] * stats_ref[2:3, columns] + scales[1] * stats_ref[10:11, columns]
            delta = delta / total
            share = jnp.where(core == 0, scales[0], scales[1]) / total
            e = e_ref[at, columns].astype(jnp.float32) * share
            en = e.astype(jnp.bfloat16)
            ds = (e * (dp_ref[at, columns] - delta)).astype(jnp.bfloat16)
            dk = dk + lax.dot_general(ds, q, NN, preferred_element_type=jnp.float32)
            dv = dv + lax.dot_general(en, do, NN, preferred_element_type=jnp.float32)
            en_ref[at, columns] = en
            ds_ref[at, columns] = ds
        grad_ref[at, :HD] = (dk * SCALE).astype(jnp.bfloat16)
        grad_ref[at, HD:] = dv.astype(jnp.bfloat16)


def partial(window_ref, en_ref, ds_ref, keep_ref, send_ref):
    core = lax.axis_index("ctx") % 2
    out = lax.dot_general(
        window_ref[:, HD:].T, en_ref[...], NN, preferred_element_type=jnp.float32
    )
    dq = SCALE * lax.dot_general(
        window_ref[:, :HD].T, ds_ref[...], NN, preferred_element_type=jnp.float32
    )
    for at, both in ((0, out), (HD, dq)):
        one, two = both[:, :COLS], both[:, COLS:]
        keep_ref[at : at + HD, :] = jnp.where(core == 0, one, two)
        send_ref[at : at + HD, :] = jnp.where(core == 0, two, one).astype(jnp.bfloat16)


def finish(sent_ref, keep_ref, out_ref, dq_ref, far_out_ref):
    core = lax.axis_index("ctx") % 2
    came = sent_ref[pl.ds(pl.multiple_of((1 - core) * 2 * HD, 2 * HD), 2 * HD), :]
    both = (keep_ref[...] + came.astype(jnp.float32)).astype(jnp.bfloat16)
    out = both[:HD].T
    dq = both[HD:].T
    for h in range(N_HEAD):
        part = slice(h * HD, (h + 1) * HD)
        own = slice(h * STRETCH, (h + 1) * STRETCH)
        far = slice((h + N_HEAD) * STRETCH, (h + N_HEAD + 1) * STRETCH)
        out_ref[:, part] = out[own]
        dq_ref[:, part] = dq[own]
        far_out_ref[:STRETCH, part] = out[far]
        far_out_ref[STRETCH:, part] = dq[far]


VMEM = pl.BlockSpec(memory_space=pltpu.VMEM)
SMEM = pl.BlockSpec(memory_space=pltpu.SMEM)
F32 = jnp.float32


def shaped(rows, columns, dtype=jnp.bfloat16):
    return jax.ShapeDtypeStruct((rows, columns), dtype)


def run(kernel, outs, args, flops, scratch=(), scalars=0):
    return pl.pallas_call(
        kernel,
        out_shape=outs,
        in_specs=[SMEM] * scalars + [VMEM] * (len(args) - scalars),
        out_specs=(VMEM,) * len(outs),
        scratch_shapes=scratch,
        compiler_params=pltpu.CompilerParams(vmem_limit_bytes=20 << 20),
        cost_estimate=pl.CostEstimate(flops=flops, bytes_accessed=8 * COLS * HD, transcendentals=0),
    )(*args)


def settled(*arrays):
    wide, thin = shaped(2 * STRETCH, N_HEAD * HD), shaped(2 * STRETCH, HD)
    return pl.pallas_call(
        settle,
        out_shape=(wide, wide, thin, thin),
        in_specs=[VMEM] * 4,
        out_specs=(pl.BlockSpec(memory_space=pltpu.HBM),) * 4,
        scratch_shapes=(pltpu.SemaphoreType.DMA((6,)),),
        compiler_params=pltpu.CompilerParams(vmem_limit_bytes=2 << 20),
    )(*arrays)


def bounded(docs):
    return run(bounds, (shaped(8, 2 * COLS, jnp.int32),), (docs,), DOCS * COLS, scalars=1)[0]


def prepared(query, grad, far):
    return run(prepare, (shaped(2 * COLS, HD),), (query, grad, far), COLS * HD)[0]


def scored(window, both, begin):
    outs = (shaped(SIDE, 2 * COLS), shaped(SIDE, 2 * COLS, F32), shaped(8, 2 * COLS, F32))
    work = 8 * SIDE * COLS * HD
    return run(score, outs, (window, both, begin), work, (pltpu.VMEM((SIDE, 2 * COLS), F32),))


def graded(window, both, e, dp, stats):
    outs = (shaped(SIDE, 2 * HD), shaped(SIDE, 2 * COLS), shaped(SIDE, 2 * COLS))
    return run(grads, outs, (window, both, e, dp, stats), 8 * SIDE * COLS * HD)


def parted(window, en, ds):
    outs = (shaped(2 * HD, COLS, F32), shaped(2 * HD, COLS))
    return run(partial, outs, (window, en, ds), 8 * SIDE * COLS * HD)


def finished(sent, keep):
    half, both = shaped(STRETCH, N_HEAD * HD), shaped(2 * STRETCH, N_HEAD * HD)
    return run(finish, (half, half, both), (sent, keep), COLS * HD)


def paired(array, axis="ctx", groups=PAIRS):
    return lax.all_gather(array, axis, axis_index_groups=groups, axis=0, tiled=True)


def body(query, key, value, grad_out, doc_lengths):
    lower = lax.axis_index("head") < N_HEAD // 2
    mine = jnp.where(lower, 0, STRETCH)

    def pick(first, second, start):
        both = jnp.concatenate([first, second], axis=1)
        return lax.dynamic_slice_in_dim(both, start, STRETCH, 0)

    own = pick(key, value, mine)
    far = across(pick(query, grad_out, STRETCH - mine))
    at_4 = along(own, 4 * CHIP)
    two = jnp.concatenate([own, at_4], axis=0)
    at_2_6 = along(two, 2 * CHIP)
    at_8 = along(at_4, 4 * CHIP)
    four = jnp.concatenate([two, at_2_6], axis=0)
    odd = along(four, CHIP)
    parity = jnp.concatenate([four, odd, at_8], axis=0)
    begin = bounded(doc_lengths)
    own_rows = prepared(query, grad_out, far)
    both = paired(own_rows)
    e, dp, stats = scored(parity, both, begin)
    stats = paired(stats)
    grad, en, ds = graded(parity, both, e, dp, stats)
    keep, send = parted(parity, en, ds)
    out, dq, far_out = finished(paired(send), keep)

    def block(start, stop):
        return grad[start * STRETCH : stop * STRETCH]

    def home_by(array, chips):
        return along(array.astype(jnp.bfloat16), -chips * CHIP).astype(jnp.float32)

    eighth = home_by(block(8, 9), 4)
    even = block(0, 4).astype(F32) + home_by(block(4, 8), 1)
    first = even[: 2 * STRETCH] + home_by(even[2 * STRETCH :], 2)
    back = across(far_out)
    total = (first[:STRETCH] + home_by(first[STRETCH:] + eighth, 4)).astype(jnp.bfloat16)
    copies = jnp.broadcast_to(total, (N_HEAD,) + total.shape)
    shared = lax.all_to_all(copies, "head", 0, 0).astype(F32)
    kv = jnp.concatenate([shared[0] + shared[1], shared[2] + shared[3]], axis=0)
    kv = kv.astype(jnp.bfloat16)
    return settled(out, dq, back, kv)


def solution(mesh):
    in_specs = (P("ctx", "head"), P("ctx", None), P("ctx", None), P("ctx", "head"), P())
    out_specs = (P("ctx", "head"), P("ctx", "head"), P("ctx", None), P("ctx", None))

    return jax.shard_map(body, mesh=mesh, in_specs=in_specs, out_specs=out_specs, check_vma=False)
```
